32 devices in a mesh: ha: 8 (over y, x, core), col: 4 (over z).
Axes of the slice: x: 2, y: 2, z: 4, core: 2. Of those that a mesh axis runs over, the one named last changes fastest.
Arguments:
- features: bfloat16 [3, 32, 128, 512], P(None, 'ha', 'col'), may hold values from -18 to 18
Outputs:
- lag_cov: float32 [128, 16000], P('col', 'ha')
The draws below stay inside these ranges and needn't reach their ends.
All inputs are finite; a program needn't handle non-finite values.
Results may differ from the reference program's by a relative error of at most 0.0003.
Values may be sent and summed in bfloat16 or wider, within the bound.
A program may use at most 384 MiB of HBM per device.

```python
import jax
import jax.numpy as jnp
from jax import lax

C = 128
W = 512
TF = 3
H = 32


def draw_features(key, part):
    keys = jax.random.split(key, 9)
    rough_field = jnp.clip(jax.random.normal(keys[0], (TF, H, C, W), jnp.float32), -5.0, 5.0)
    weight_scale = 0.6
    mix_spread = 0.5
    loads = jnp.clip(jax.random.normal(keys[1], (6, C), jnp.float32) * weight_scale, -1.5, 1.5)
    wave_w = jax.random.uniform(keys[2], (6,), jnp.float32, 0.05, 0.9)
    wave_h = jax.random.uniform(keys[3], (6,), jnp.float32, 0.05, 0.9)
    wave_t = jax.random.uniform(keys[4], (6,), jnp.float32, 0.2, 1.5)
    phases = jax.random.uniform(keys[5], (6,), jnp.float32, 0.0, 6.2831853)
    frame_pos = jnp.arange(TF, dtype=jnp.float32)[:, None, None, None]
    row_pos = jnp.arange(H, dtype=jnp.float32)[None, :, None, None]
    column_pos = jnp.arange(W, dtype=jnp.float32)[None, None, None, :]
    kernels = jax.random.normal(keys[6], (27, C), jnp.float32) * 0.19245
    padded_rough = jnp.pad(rough_field, ((1, 1), (1, 1), (0, 0), (1, 1)))
    smooth_field = jnp.zeros((TF, H, C, W), jnp.float32)
    tap_index = 0
    for step_t in range(3):
        for step_h in range(3):
            for step_w in range(3):
                smooth_field = smooth_field + kernels[tap_index][None, None, :, None] * padded_rough[step_t:step_t + TF, step_h:step_h + H, :, step_w:step_w + W]
                tap_index = tap_index + 1
    groups = C // 8
    inner_mix = jnp.eye(8, dtype=jnp.float32)[None, :, :] + mix_spread * 0.35355 * jax.random.normal(keys[7], (groups, 8, 8), jnp.float32)
    outer_mix = jnp.eye(groups, dtype=jnp.float32)[None, :, :] + mix_spread * groups ** (-0.5) * jax.random.normal(keys[8], (8, groups, groups), jnp.float32)
    grouped = smooth_field.reshape(TF, H, groups, 8, W)
    section_mix = jnp.zeros((TF, H, groups, 8, W), jnp.float32)
    for source in range(8):
        section_mix = section_mix + inner_mix[:, :, source][None, None, :, :, None] * grouped[:, :, :, source:source + 1, :]
    mixed_field = jnp.zeros((TF, H, groups, 8, W), jnp.float32)
    for source in range(groups):
        outer_column = jnp.transpose(outer_mix[:, :, source], (1, 0))
        mixed_field = mixed_field + outer_column[None, None, :, :, None] * section_mix[:, :, source:source + 1, :, :]
    result = 1.5 * mixed_field.reshape(TF, H, C, W)
    for component in range(6):
        angle_field = wave_w[component] * column_pos + wave_h[component] * row_pos + wave_t[component] * frame_pos + phases[component]
        result = result + 1.4142 * loads[component][None, None, :, None] * jnp.cos(angle_field)
    return jnp.clip(result, -18.0, 18.0).astype(jnp.bfloat16)


def setup_inputs(seed: int = 0) -> dict:
    key_list = jax.random.split(jax.random.key(seed), 2)
    features = draw_features(jax.random.fold_in(key_list[1], 71), 0)
    return dict(features=features)


def reference(features):
    fields = jnp.transpose(features.astype(jnp.float32), (2, 0, 1, 3))
    own_rows = fields.reshape(C, -1)
    padded = jnp.pad(fields, ((0, 0), (2, 2), (2, 2), (2, 2)))
    position_count = TF * H * W

    def lag_cov(lag_index):
        step_t = lag_index // 25
        step_h = (lag_index // 5) % 5
        step_w = lag_index % 5
        zero_index = jnp.zeros((), jnp.int32)
        shifted = lax.dynamic_slice(padded, (zero_index, step_t.astype(jnp.int32), step_h.astype(jnp.int32), step_w.astype(jnp.int32)), (C, TF, H, W))
        other_rows = shifted.reshape(C, -1)
        return jnp.dot(own_rows, other_rows.T, precision=lax.Precision.HIGHEST, preferred_element_type=jnp.float32) / position_count

    blocks = lax.map(lag_cov, jnp.arange(125, dtype=jnp.int32))
    return jnp.transpose(blocks, (1, 0, 2)).reshape(C, 125 * C)
```

```python
import functools

import jax
import jax.numpy as jnp
from jax import lax
from jax.experimental import pallas as pl
from jax.experimental.pallas import tpu as pltpu
from jax.sharding import PartitionSpec as P

MESH = pl.DeviceIdType.MESH
REACH = 2
STEPS = 2 * REACH + 1


def window_plan(lag_count, channels, ha_count):
    share = lag_count * channels // ha_count
    spans = [-(-(i + 1) * share // channels) - i * share // channels for i in range(ha_count)]
    return share, max(spans)


def kernel(
    ha_count, col_count, x_ref, out_ref, stack, others, acc, part, near, mixed, far, summed, direct, turned,
    edges, edge_left, edge_own,
    local_sem, halo_send, halo_recv, line_send, line_recv, near_send, near_recv, far_send, far_recv,
    direct_send, direct_recv, turned_send, turned_recv, edge_send, edge_recv,
):
    frames, rows, block, width = x_ref.shape
    channels = block * col_count
    lag_count = STEPS**3
    share, span = window_plan(lag_count, channels, ha_count)
    i, j = lax.axis_index("ha"), lax.axis_index("col")
    half = ha_count // 2
    parity, place = lax.rem(i, 2), lax.div(i, 2)
    partner = i + 1 - 2 * parity
    mirror = ha_count - 1 - i
    middle = col_count // 2
    cut = width // 2
    frame_rows = frames * block

    def first_lag(index):
        return jnp.minimum(lax.div(index * share, channels), lag_count - span)

    barrier = pltpu.get_barrier_semaphore()
    for step in range(1, ha_count):
        pl.semaphore_signal(
            barrier, inc=1, device_id={"ha": lax.rem(i + step, ha_count)}, device_id_type=MESH
        )

    @pl.when(j > 0)
    def _():
        pl.semaphore_signal(barrier, inc=1, device_id={"col": j - 1}, device_id_type=MESH)

    @pl.when(j < col_count - 1)
    def _():
        pl.semaphore_signal(barrier, inc=1, device_id={"col": j + 1}, device_id_type=MESH)

    own_copies = [
        pltpu.make_async_copy(x_ref.at[:, h], stack.at[REACH + h, REACH], local_sem.at[h])
        for h in range(rows)
    ]
    for copy in own_copies:
        copy.start()

    ends = (j > 0).astype(jnp.int32) + (j < col_count - 1).astype(jnp.int32)
    pl.semaphore_wait(barrier, ha_count - 1 + ends)

    def halo(way, r):
        source = rows - REACH + r if way == 0 else r
        slot = r if way == 0 else rows + REACH + r
        return pltpu.make_async_remote_copy(
            src_ref=x_ref.at[:, source],
            dst_ref=stack.at[slot, REACH],
            send_sem=halo_send.at[way, r],
            recv_sem=halo_recv.at[way, r],
            device_id={"ha": (i + 1) if way == 0 else (i - 1)},
            device_id_type=MESH,
        )

    rest = max(col_count - 1, 1)

    def lanes_of(way):
        return pl.ds(cut, cut) if way == 0 else pl.ds(0, cut)

    def hop(way, step, h):
        sign = 1 if way == 0 else -1
        fresh = step in (0, rest)
        owner = j if fresh else j - sign * step
        lanes = lanes_of(1 - way if step == rest else way)
        return pltpu.make_async_remote_copy(
            src_ref=x_ref.at[:, h, :, lanes] if fresh else others.at[owner, h, :, :, lanes],
            dst_ref=others.at[owner, h, :, :, lanes],
            send_sem=line_send.at[way, step, h],
            recv_sem=line_recv.at[way, step, h],
            device_id={"col": j + sign},
            device_id_type=MESH,
        )

    def edge_hop(step):
        return pltpu.make_async_remote_copy(
            src_ref=edges.at[j - step],
            dst_ref=edges.at[j - step],
            send_sem=edge_send.at[step],
            recv_sem=edge_recv.at[step],
            device_id={"col": j + 1},
            device_id_type=MESH,
        )

    def edge_arrival(step):
        owner = j - 1 - step
        return pltpu.make_async_remote_copy(
            src_ref=edges.at[owner],
            dst_ref=edges.at[owner],
            send_sem=edge_send.at[step],
            recv_sem=edge_recv.at[step],
            device_id={"col": j - 1},
            device_id_type=MESH,
        )

    def travels(way, owner):
        if way == 0:
            useful = True if col_count - 2 < middle else owner != col_count - 2
            return jnp.logical_and(owner >= 0, useful)
        useful = True if 1 >= middle else owner != 1
        return jnp.logical_and(owner <= col_count - 1, useful)

    def sends(way, step):
        if way == 0:
            return jnp.logical_and(j < col_count - 1, travels(0, j - step))
        return jnp.logical_and(j > 0, travels(1, j + step))

    def receives(way, step):
        return travels(0, j - 1 - step) if way == 0 else travels(1, j + 1 + step)

    def sends_rest(way):
        return j + 1 < middle if way == 0 else j - 1 >= middle

    def receives_rest(way):
        if way == 0:
            return jnp.logical_and(j >= 1, j < middle)
        return jnp.logical_and(j >= middle, j < col_count - 1)

    def arrival(way, step, h):
        sign = 1 if way == 0 else -1
        owner = j - sign * (1 if step == rest else step + 1)
        lanes = lanes_of(1 - way if step == rest else way)
        return pltpu.make_async_remote_copy(
            src_ref=others.at[owner, h, :, :, lanes],
            dst_ref=others.at[owner, h, :, :, lanes],
            send_sem=line_send.at[way, step, h],
            recv_sem=line_recv.at[way, step, h],
            device_id={"col": j - sign},
            device_id_type=MESH,
        )

    for way in range(2):

        @pl.when(sends(way, 0))
        def _():
            for h in range(rows):
                hop(way, 0, h).start()

    has_after, has_before = i < ha_count - 1, i > 0
    for way, has in ((0, has_after), (1, has_before)):

        @pl.when(has)
        def _():
            for r in range(REACH):
                halo(way, r).start()

    for way in range(2):

        @pl.when(sends_rest(way))
        def _():
            for h in range(rows):
                hop(way, rest, h).start()

    inner = jnp.minimum(j, col_count - 1 - j) >= 1
    low = j < middle
    same_side = jnp.where(low, j + 1 < middle, j - 1 >= middle)
    inward = jnp.where(low, 1, -1)
    both = jnp.minimum(j, col_count - 1 - j)

    def owner_of(slot):
        if slot == 0:
            return j
        paired = j + ((slot + 1) // 2) * (inward if slot % 2 == 1 else -inward)
        single = j + inward * (slot - both)
        return jnp.where(slot <= 2 * both, paired, single)

    def when_active(slot, action):
        if slot == 1:
            pl.when(jnp.logical_not(same_side))(action)
        else:
            action()

    for slot in range(col_count):
        owner = owner_of(slot)
        blank = jnp.zeros(direct.shape[1:], direct.dtype)
        if slot == 0:
            turned[owner] = blank
        elif slot == 1:

            @pl.when(same_side)
            def _():
                turned[owner] = blank

        elif slot == 2:

            @pl.when(inner)
            def _():
                direct[owner] = blank

    column = lax.broadcasted_iota(jnp.int32, (block, width), 1)

    def shift_row(row, t):
        plain = stack[row, REACH, t]
        wide = plain.astype(jnp.float32)
        for step_w in range(STEPS):
            shift = REACH - step_w
            if shift != 0:
                moved = pltpu.roll(wide, shift % width, axis=1)
                keep = column >= shift if shift > 0 else column < width + shift
                stack[row, step_w, t] = jnp.where(keep, moved, 0.0).astype(plain.dtype)

    def shift_rows(first, count):
        def step(index, carry):
            shift_row(first + lax.div(index, frames), lax.rem(index, frames))
            return carry

        lax.fori_loop(0, count * frames, step, 0)

    for copy in own_copies:
        copy.wait()

    edge_tile = pl.ds(cut - channels, channels)
    edge_lane = lax.broadcasted_iota(jnp.int32, (frame_rows, channels), 1)

    def gather_edge(field, count):
        total = jnp.zeros((frame_rows, channels), jnp.float32)
        for h in range(count):
            tile = field(h).reshape(frame_rows, channels).astype(jnp.float32)
            moved = pltpu.roll(tile, (REACH * (h + 1)) % channels, axis=1)
            total = jnp.where(edge_lane // REACH == h, moved, total)
        return total

    @pl.when(sends(0, 0))
    def _():
        own_edge = gather_edge(lambda h: stack[REACH + h, REACH, :, :, edge_tile], rows)
        edges[j] = own_edge.astype(edges.dtype).reshape(frames, block, channels)
        edge_hop(0).start()

    shift_rows(REACH, rows)

    def advance(step, part_rows):
        for h in part_rows:
            for way in range(2):

                @pl.when(receives(way, step))
                def _():
                    arrival(way, step, h).wait_recv()

                if step + 1 < col_count - 1:

                    @pl.when(sends(way, step + 1))
                    def _():
                        hop(way, step + 1, h).start()

        if part_rows[-1] == rows - 1:

            @pl.when(receives(0, step))
            def _():
                edge_arrival(step).wait_recv()

            if step + 1 < col_count - 1:

                @pl.when(sends(0, step + 1))
                def _():
                    edge_hop(step + 1).start()

    halves = list(range(rows))
    if col_count > 1:
        advance(0, halves)

    for way, has_in, place_row in ((0, has_before, 0), (1, has_after, rows + REACH)):

        @pl.when(has_in)
        def _():
            for r in range(REACH):
                halo(way, r).wait_recv()
            shift_rows(place_row, REACH)

        @pl.when(jnp.logical_not(has_in))
        def _():
            for r in range(REACH):
                stack[place_row + r] = jnp.zeros(stack.shape[1:], stack.dtype)

    group = block // col_count
    scale = 1.0 / (frames * rows * ha_count * width)
    lane_block = lax.broadcasted_iota(jnp.int32, (group, channels), 1) // block

    def products(field, lanes, depth):
        for r in range(rows + 2 * REACH):
            picked = range(max(0, r - 2 * REACH), min(rows - 1, r) + 1)
            left = jnp.concatenate([field(h).reshape(frame_rows, depth) for h in picked], axis=0)
            own = stack[r, :, :, :, lanes].reshape(STEPS * frame_rows, depth)
            result = lax.dot_general(
                left, own, (((1,), (1,)), ((), ())), preferred_element_type=jnp.float32
            )
            for place_in, h in enumerate(picked):
                piece = result[place_in * frame_rows : (place_in + 1) * frame_rows]
                outs = pl.ds(0, STEPS * frame_rows)
                if h == 0:
                    acc[r - h, :, outs] = piece
                else:
                    acc[r - h, :, outs] = acc[r - h, :, outs] + piece

    edge_first = (STEPS - REACH) * frame_rows // channels * channels
    edge_pad = (STEPS - REACH) * frame_rows - edge_first
    edge_outs = pl.ds(edge_first, STEPS * frame_rows - edge_first)

    def gather_own_edges():
        if edge_pad:
            edge_own[:edge_pad] = jnp.zeros((edge_pad, channels), edge_own.dtype)
        for step_w in range(STEPS - REACH, STEPS):
            found = gather_edge(lambda r: stack[r, step_w, :, :, edge_tile], rows + 2 * REACH)
            kept = jnp.where(edge_lane % REACH >= 2 * REACH - step_w, found, 0.0)
            row = edge_pad + (step_w - STEPS + REACH) * frame_rows
            edge_own[row : row + frame_rows] = kept.astype(edge_own.dtype)

    def add_edges(owner):
        @pl.when(owner < j)
        def _():
            edge_left[...] = edges[owner].reshape(frame_rows, channels).astype(jnp.float32)

        @pl.when(owner > j)
        def _():
            edge_left[...] = -gather_edge(lambda h: others[owner, h, :, :, edge_tile], rows)

        plain = edge_left[...]
        turned_edges = [plain] + [pltpu.roll(plain, REACH * b, axis=1) for b in range(1, STEPS)]
        left = jnp.concatenate([edge.astype(edge_own.dtype) for edge in turned_edges], axis=0)
        result = lax.dot_general(
            left, edge_own[...], (((1,), (1,)), ((), ())), preferred_element_type=jnp.float32
        )
        for b in range(STEPS):
            acc[b, :, edge_outs] = acc[b, :, edge_outs] + result[b * frame_rows : (b + 1) * frame_rows]

    def pack(slot):
        def step(step_h, carry):
            moved = []
            for tile in range(acc.shape[2] // channels):
                plain = acc[step_h, :, tile * channels : (tile + 1) * channels] * scale
                moved.append([plain] + [pltpu.roll(plain, k * block, axis=1) for k in range(1, col_count)])
            for step_w in range(STEPS):
                for step_t in range(STEPS):
                    shift = step_t - REACH
                    packed = None
                    for g in range(col_count):
                        total = None
                        for t in range(frames):
                            if 0 <= t + shift < frames:
                                spot = step_w * frames + t + shift
                                row = t * block + g * group
                                source = moved[spot // col_count][(g - spot) % col_count]
                                term = source[row : row + group]
                                total = term if total is None else total + term
                        if total is None:
                            total = jnp.zeros((group, channels), jnp.float32)
                        packed = total if packed is None else jnp.where(lane_block == g, total, packed)
                    part[slot, step_t * STEPS * STEPS + step_h * STEPS + step_w] = packed
            return carry

        lax.fori_loop(0, STEPS, step, 0)

    def half_slot(owner):
        lanes = pl.ds(pl.multiple_of(jnp.where(owner < j, cut, 0), cut), cut)
        products(lambda h: others[owner, h, :, :, lanes], lanes, cut)
        add_edges(owner)

    turns = [*range(1, half), 0]

    def near_copy(slot, r):
        target = lax.rem(place + r, half)
        return pltpu.make_async_remote_copy(
            src_ref=part.at[slot, pl.ds(first_lag(2 * target + 1 - parity), span)],
            dst_ref=near.at[slot, r],
            send_sem=near_send.at[slot, r],
            recv_sem=near_recv.at[slot, r],
            device_id={"ha": partner},
            device_id_type=MESH,
        )

    def far_copy(slot, r):
        target = lax.rem(place + r, half)
        return pltpu.make_async_remote_copy(
            src_ref=mixed.at[slot, r],
            dst_ref=far.at[slot, r - 1],
            send_sem=far_send.at[slot, r - 1],
            recv_sem=far_recv.at[slot, r - 1],
            device_id={"ha": 2 * target + parity},
            device_id_type=MESH,
        )

    def direct_copy(slot):
        owner = owner_of(slot)
        return pltpu.make_async_remote_copy(
            src_ref=summed.at[slot],
            dst_ref=direct.at[j],
            send_sem=direct_send.at[slot],
            recv_sem=direct_recv.at[j],
            device_id={"col": owner},
            device_id_type=MESH,
        )

    def direct_arrival(owner):
        return pltpu.make_async_remote_copy(
            src_ref=direct.at[owner],
            dst_ref=direct.at[owner],
            send_sem=direct_send.at[0],
            recv_sem=direct_recv.at[owner],
            device_id={"col": owner},
            device_id_type=MESH,
        )

    def turned_copy(slot):
        owner = owner_of(slot)
        return pltpu.make_async_remote_copy(
            src_ref=summed.at[slot],
            dst_ref=turned.at[owner],
            send_sem=turned_send.at[slot],
            recv_sem=turned_recv.at[slot],
            device_id={"ha": mirror},
            device_id_type=MESH,
        )

    def pass_near(slot):
        def action():
            for r in turns:
                near_copy(slot, r).start()

        when_active(slot, action)

    def pass_far(slot):
        def action():
            for r in turns:
                target = lax.rem(place + r, half)
                near_copy(slot, r).wait_recv()
                mixed[slot, r] = part[slot, pl.ds(first_lag(2 * target + parity), span)] + near[slot, r]
                if r > 0:
                    far_copy(slot, r).start()

        when_active(slot, action)

    def finish(slot):
        def action():
            total = mixed[slot, 0]
            for r in range(1, half):
                far_copy(slot, r).wait_recv()
                total = total + far[slot, r - 1]
            if slot == 0:
                direct[j] = total
            else:
                summed[slot] = total
                direct_copy(slot).start()
                turned_copy(slot).start()

        when_active(slot, action)

    products(lambda h: stack[REACH + h, REACH], pl.ds(0, width), width)
    if col_count > 2:
        advance(1, halves[: rows // 2])
    pack(0)
    pass_near(0)
    gather_own_edges()
    for slot in range(1, col_count):
        owner = owner_of(slot)
        if slot == 1:

            @pl.when(jnp.logical_not(same_side))
            def _():
                half_slot(owner)
                pack(slot)

            if col_count > 2:
                advance(1, halves[rows // 2 :])
        elif slot == 2:
            for way in range(2):

                @pl.when(receives_rest(way))
                def _():
                    for h in range(rows):
                        arrival(way, rest, h).wait_recv()

            @pl.when(inner)
            def _():
                products(lambda h: others[owner, h], pl.ds(0, width), width)

            @pl.when(jnp.logical_not(inner))
            def _():
                half_slot(owner)

            pack(slot)
        else:
            advance(slot - 1, halves)
            half_slot(owner)
            pack(slot)
        pass_near(slot)
        pass_far(slot - 1)
        if slot > 1:
            finish(slot - 2)
    if col_count > 1:
        pass_far(col_count - 1)
        finish(col_count - 2)
    finish(col_count - 1)

    def assemble(ref, index):
        tiles = [ref[q, index] for q in range(col_count)]
        lines = []
        for g in range(col_count):
            line = None
            for q in range(col_count):
                turn = (q - g) * block % channels
                tile = pltpu.roll(tiles[q], turn, axis=1) if turn else tiles[q]
                line = tile if line is None else jnp.where(lane_block == q, tile, line)
            lines.append(line)
        return lines

    for slot in range(1, col_count):
        owner = owner_of(slot)
        if slot == 2:
            pl.when(jnp.logical_not(inner))(lambda: direct_arrival(owner).wait_recv())
        else:
            direct_arrival(owner).wait_recv()
        when_active(slot, lambda: turned_copy(slot).wait_recv())

    reach_index = lag_count - 1 - first_lag(i) - first_lag(mirror)
    for base in range(0, span, col_count):
        taken = range(base, min(base + col_count, span))
        lines = []
        for k in taken:
            lines.extend(assemble(turned, jnp.clip(reach_index - k, 0, span - 1)))
        lines.extend([jnp.zeros((group, channels), jnp.float32)] * (channels // group - len(lines)))
        flipped = jnp.concatenate(lines, axis=0).T
        for at, k in enumerate(taken):
            plain = assemble(direct, k)
            for g in range(col_count):
                line = None
                for q in range(col_count):
                    row = q * block + g * group
                    turn = (q - at) * block % channels
                    tile = flipped[row : row + group]
                    tile = pltpu.roll(tile, turn, axis=1) if turn else tile
                    line = tile if line is None else jnp.where(lane_block == q, tile, line)
                out_ref[g * group : (g + 1) * group, k * channels : (k + 1) * channels] = plain[g] + line

    def settle(slot):
        def action():
            for r in turns:
                near_copy(slot, r).wait_send()
                if r > 0:
                    far_copy(slot, r).wait_send()
            if slot > 0:
                direct_copy(slot).wait_send()
                turned_copy(slot).wait_send()

        when_active(slot, action)

    for slot in range(col_count):
        settle(slot)
    for way in range(2):
        for step in range(col_count - 1):

            @pl.when(sends(way, step))
            def _():
                for h in range(rows):
                    hop(way, step, h).wait_send()

        @pl.when(sends_rest(way))
        def _():
            for h in range(rows):
                hop(way, rest, h).wait_send()

    for step in range(col_count - 1):

        @pl.when(sends(0, step))
        def _():
            edge_hop(step).wait_send()

    for way, has in ((0, has_after), (1, has_before)):

        @pl.when(has)
        def _():
            for r in range(REACH):
                halo(way, r).wait_send()


def body(ha_count, col_count, features):
    frames, rows, block, width = features.shape
    channels = block * col_count
    lag_count = STEPS**3
    share, span = window_plan(lag_count, channels, ha_count)
    half = ha_count // 2
    group = block // col_count
    dma = pltpu.SemaphoreType.DMA
    lines = max(col_count - 1, 1)
    lanes = -(-STEPS * frames * block // channels) * channels
    tiles = pltpu.VMEM((col_count, span, group, channels), jnp.float32)
    edge_first = (STEPS - REACH) * frames * block // channels * channels
    window = pl.pallas_call(
        functools.partial(kernel, ha_count, col_count),
        out_shape=pltpu.VMEM((block, span * channels), jnp.float32),
        in_specs=[pl.BlockSpec(memory_space=pl.ANY)],
        out_specs=pl.BlockSpec(memory_space=pltpu.VMEM),
        scratch_shapes=[
            pltpu.VMEM((rows + 2 * REACH, STEPS, frames, block, width), features.dtype),
            pltpu.VMEM((col_count, rows, frames, block, width), features.dtype),
            pltpu.VMEM((STEPS, frames * block, lanes), jnp.float32),
            pltpu.VMEM((col_count, lag_count, group, channels), jnp.float32),
            pltpu.VMEM((col_count, half, span, group, channels), jnp.float32),
            pltpu.VMEM((col_count, half, span, group, channels), jnp.float32),
            pltpu.VMEM((col_count, half, span, group, channels), jnp.float32),
            tiles,
            tiles,
            tiles,
            pltpu.VMEM((col_count, frames, block, channels), features.dtype),
            pltpu.VMEM((frames * block, channels), jnp.float32),
            pltpu.VMEM((STEPS * frames * block - edge_first, channels), features.dtype),
            dma((rows,)),
            dma((2, REACH)),
            dma((2, REACH)),
            dma((2, lines + 1, rows)),
            dma((2, lines + 1, rows)),
            dma((col_count, half)),
            dma((col_count, half)),
            dma((col_count, half)),
            dma((col_count, half)),
            dma((col_count,)),
            dma((col_count,)),
            dma((col_count,)),
            dma((col_count,)),
            dma((lines,)),
            dma((lines,)),
        ],
        compiler_params=pltpu.CompilerParams(collective_id=0, has_side_effects=True),
        name="lag_cov",
    )(features)
    i = lax.axis_index("ha")
    first = jnp.minimum(i * share // channels, lag_count - span)
    return lax.dynamic_slice_in_dim(window, i * share - first * channels, share, 1)


def solution(mesh):
    in_specs = (P(None, "ha", "col", None),)
    out_specs = P("col", "ha")
    counts = (mesh.shape["ha"], mesh.shape["col"])
    return jax.shard_map(
        functools.partial(body, *counts), mesh=mesh, in_specs=in_specs, out_specs=out_specs, check_vma=False
    )
```

```python
import functools

import jax
import jax.numpy as jnp
from jax import lax
from jax.experimental import pallas as pl
from jax.experimental.pallas import tpu as pltpu
from jax.sharding import PartitionSpec as P

MESH = pl.DeviceIdType.MESH
REACH = 2
STEPS = 2 * REACH + 1


def window_plan(lag_count, channels, ha_count):
    share = lag_count * channels // ha_count
    spans = [-(-(i + 1) * share // channels) - i * share // channels for i in range(ha_count)]
    return share, max(spans)


def kernel(
    ha_count, col_count, x_ref, out_ref, stack, others, acc, part, near, mixed, far, summed, direct, turned,
    edges, edge_left, edge_own,
    local_sem, halo_send, halo_recv, line_send, line_recv, near_send, near_recv, far_send, far_recv,
    direct_send, direct_recv, turned_send, turned_recv, edge_send, edge_recv,
):
    frames, rows, block, width = x_ref.shape
    channels = block * col_count
    lag_count = STEPS**3
    share, span = window_plan(lag_count, channels, ha_count)
    i, j = lax.axis_index("ha"), lax.axis_index("col")
    half = ha_count // 2
    parity, place = lax.rem(i, 2), lax.div(i, 2)
    partner = i + 1 - 2 * parity
    mirror = ha_count - 1 - i
    middle = col_count // 2
    cut = width // 2
    frame_rows = frames * block

    def first_lag(index):
        return jnp.minimum(lax.div(index * share, channels), lag_count - span)

    barrier = pltpu.get_barrier_semaphore()
    for step in range(1, ha_count):
        pl.semaphore_signal(
            barrier, inc=1, device_id={"ha": lax.rem(i + step, ha_count)}, device_id_type=MESH
        )

    @pl.when(j > 0)
    def _():
        pl.semaphore_signal(barrier, inc=1, device_id={"col": j - 1}, device_id_type=MESH)

    @pl.when(j < col_count - 1)
    def _():
        pl.semaphore_signal(barrier, inc=1, device_id={"col": j + 1}, device_id_type=MESH)

    own_copies = [
        pltpu.make_async_copy(x_ref.at[:, h], stack.at[REACH + h, REACH], local_sem.at[h])
        for h in range(rows)
    ]
    for copy in own_copies:
        copy.start()

    ends = (j > 0).astype(jnp.int32) + (j < col_count - 1).astype(jnp.int32)
    pl.semaphore_wait(barrier, ha_count - 1 + ends)

    def halo(way, r):
        source = rows - REACH + r if way == 0 else r
        slot = r if way == 0 else rows + REACH + r
        return pltpu.make_async_remote_copy(
            src_ref=x_ref.at[:, source],
            dst_ref=stack.at[slot, REACH],
            send_sem=halo_send.at[way, r],
            recv_sem=halo_recv.at[way, r],
            device_id={"ha": (i + 1) if way == 0 else (i - 1)},
            device_id_type=MESH,
        )

    rest = max(col_count - 1, 1)

    def lanes_of(way):
        return pl.ds(cut, cut) if way == 0 else pl.ds(0, cut)

    def hop(way, step, h):
        sign = 1 if way == 0 else -1
        fresh = step in (0, rest)
        owner = j if fresh else j - sign * step
        lanes = lanes_of(1 - way if step == rest else way)
        return pltpu.make_async_remote_copy(
            src_ref=x_ref.at[:, h, :, lanes] if fresh else others.at[owner, h, :, :, lanes],
            dst_ref=others.at[owner, h, :, :, lanes],
            send_sem=line_send.at[way, step, h],
            recv_sem=line_recv.at[way, step, h],
            device_id={"col": j + sign},
            device_id_type=MESH,
        )

    def edge_hop(step):
        return pltpu.make_async_remote_copy(
            src_ref=edges.at[j - step],
            dst_ref=edges.at[j - step],
            send_sem=edge_send.at[step],
            recv_sem=edge_recv.at[step],
            device_id={"col": j + 1},
            device_id_type=MESH,
        )

    def edge_arrival(step):
        owner = j - 1 - step
        return pltpu.make_async_remote_copy(
            src_ref=edges.at[owner],
            dst_ref=edges.at[owner],
            send_sem=edge_send.at[step],
            recv_sem=edge_recv.at[step],
            device_id={"col": j - 1},
            device_id_type=MESH,
        )

    def travels(way, owner):
        if way == 0:
            useful = True if col_count - 2 < middle else owner != col_count - 2
            return jnp.logical_and(owner >= 0, useful)
        useful = True if 1 >= middle else owner != 1
        return jnp.logical_and(owner <= col_count - 1, useful)

    def sends(way, step):
        if way == 0:
            return jnp.logical_and(j < col_count - 1, travels(0, j - step))
        return jnp.logical_and(j > 0, travels(1, j + step))

    def receives(way, step):
        return travels(0, j - 1 - step) if way == 0 else travels(1, j + 1 + step)

    def sends_rest(way):
        return j + 1 < middle if way == 0 else j - 1 >= middle

    def receives_rest(way):
        if way == 0:
            return jnp.logical_and(j >= 1, j < middle)
        return jnp.logical_and(j >= middle, j < col_count - 1)

    def arrival(way, step, h):
        sign = 1 if way == 0 else -1
        owner = j - sign * (1 if step == rest else step + 1)
        lanes = lanes_of(1 - way if step == rest else way)
        return pltpu.make_async_remote_copy(
            src_ref=others.at[owner, h, :, :, lanes],
            dst_ref=others.at[owner, h, :, :, lanes],
            send_sem=line_send.at[way, step, h],
            recv_sem=line_recv.at[way, step, h],
            device_id={"col": j - sign},
            device_id_type=MESH,
        )

    for way in range(2):

        @pl.when(sends(way, 0))
        def _():
            for h in range(rows):
                hop(way, 0, h).start()

    has_after, has_before = i < ha_count - 1, i > 0
    for way, has in ((0, has_after), (1, has_before)):

        @pl.when(has)
        def _():
            for r in range(REACH):
                halo(way, r).start()

    inner = jnp.minimum(j, col_count - 1 - j) >= 1
    low = j < middle
    same_side = jnp.where(low, j + 1 < middle, j - 1 >= middle)
    inward = jnp.where(low, 1, -1)
    both = jnp.minimum(j, col_count - 1 - j)

    def owner_of(slot):
        inwards = col_count - 1 - both
        return jnp.where(slot <= inwards, j + inward * slot, j - inward * (slot - inwards))

    def whole(slot):
        if 1 <= col_count - slot < middle:
            return both == col_count - slot
        return None

    def when_active(slot, action):
        if slot == 1:
            pl.when(jnp.logical_not(same_side))(action)
        else:
            action()

    blank = jnp.zeros(direct.shape[1:], direct.dtype)
    turned[j] = blank
    if col_count > 1:

        @pl.when(same_side)
        def _():
            turned[j + inward] = blank

    @pl.when(inner)
    def _():
        direct[j - inward] = blank

    frame_lane = lax.broadcasted_iota(jnp.int32, (frame_rows, channels), 1)

    def shift_rows(first, count):
        def step(index, carry):
            row = first + index
            plain = stack[row, REACH].reshape(frame_rows, width)
            for step_w in range(STEPS):
                shift = REACH - step_w
                if shift != 0:
                    moved = pltpu.roll(plain, shift % width, axis=1)
                    if shift > 0:
                        head = moved[:, :channels]
                        head = jnp.where(frame_lane >= shift, head, jnp.zeros_like(head))
                        moved = jnp.concatenate([head, moved[:, channels:]], axis=1)
                    else:
                        tail = moved[:, width - channels :]
                        tail = jnp.where(frame_lane < channels + shift, tail, jnp.zeros_like(tail))
                        moved = jnp.concatenate([moved[:, : width - channels], tail], axis=1)
                    stack[row, step_w] = moved.reshape(frames, block, width)
            return carry

        lax.fori_loop(0, count, step, 0)

    for copy in own_copies:
        copy.wait()

    edge_tile = pl.ds(cut - channels, channels)

    def gather_edge(field, count):
        total = jnp.zeros((frame_rows, channels), stack.dtype)
        for h in range(count):
            tile = field(h).reshape(frame_rows, channels)
            moved = pltpu.roll(tile, (REACH * (h + 1)) % channels, axis=1)
            total = jnp.where(frame_lane // REACH == h, moved, total)
        return total

    @pl.when(sends(0, 0))
    def _():
        own_edge = gather_edge(lambda h: stack[REACH + h, REACH, :, :, edge_tile], rows)
        edges[j] = own_edge.reshape(frames, block, channels)
        edge_hop(0).start()

    for way in range(2):

        @pl.when(sends_rest(way))
        def _():
            for h in range(rows):
                hop(way, rest, h).start()

    shift_rows(REACH, rows)

    def advance(step, part_rows):
        for h in part_rows:
            for way in range(2):

                @pl.when(receives(way, step))
                def _():
                    arrival(way, step, h).wait_recv()

                if step + 1 < col_count - 1:

                    @pl.when(sends(way, step + 1))
                    def _():
                        hop(way, step + 1, h).start()

        if rows - 1 in part_rows:

            @pl.when(receives(0, step))
            def _():
                edge_arrival(step).wait_recv()

            if step + 1 < col_count - 1:

                @pl.when(sends(0, step + 1))
                def _():
                    edge_hop(step + 1).start()

    halves = list(range(rows))
    def products(field, lanes, depth, places=None, seen=None):
        seen = set() if seen is None else seen
        for r in range(rows + 2 * REACH) if places is None else places:
            picked = range(max(0, r - 2 * REACH), min(rows - 1, r) + 1)
            left = jnp.concatenate([field(h).reshape(frame_rows, depth) for h in picked], axis=0)
            own = stack[r, :, :, :, lanes].reshape(STEPS * frame_rows, depth)
            result = lax.dot_general(
                left, own, (((1,), (1,)), ((), ())), preferred_element_type=jnp.float32
            )
            for place_in, h in enumerate(picked):
                piece = result[place_in * frame_rows : (place_in + 1) * frame_rows]
                outs = pl.ds(0, STEPS * frame_rows)
                if r - h in seen:
                    acc[r - h, :, outs] = acc[r - h, :, outs] + piece
                else:
                    acc[r - h, :, outs] = piece
                    seen.add(r - h)

    diagonal_seen = set()

    def diagonal(places):
        products(lambda h: stack[REACH + h, REACH], pl.ds(0, width), width, places, diagonal_seen)

    inside = list(range(REACH, REACH + rows))
    outside = [*range(REACH), *range(REACH + rows, rows + 2 * REACH)]
    spread = [halves[n * rows // 4 : (n + 1) * rows // 4] for n in range(4)]
    for quarter in range(3):
        if col_count > 1:
            advance(0, spread[quarter])
        if quarter < 2:
            diagonal(inside[quarter * rows // 2 : (quarter + 1) * rows // 2])

    for way, has_in, place_row in ((0, has_before, 0), (1, has_after, rows + REACH)):

        @pl.when(has_in)
        def _():
            for r in range(REACH):
                halo(way, r).wait_recv()
            shift_rows(place_row, REACH)

        @pl.when(jnp.logical_not(has_in))
        def _():
            for r in range(REACH):
                stack[place_row + r] = jnp.zeros(stack.shape[1:], stack.dtype)

    group = block // col_count
    scale = 1.0 / (frames * rows * ha_count * width)
    lane_block = lax.broadcasted_iota(jnp.int32, (group, channels), 1) // block

    edge_first = (STEPS - REACH) * frame_rows // channels * channels
    edge_pad = (STEPS - REACH) * frame_rows - edge_first
    edge_outs = pl.ds(edge_first, STEPS * frame_rows - edge_first)

    def gather_own_edges():
        if edge_pad:
            edge_own[:edge_pad] = jnp.zeros((edge_pad, channels), edge_own.dtype)
        for step_w in range(STEPS - REACH, STEPS):
            found = gather_edge(lambda r: stack[r, step_w, :, :, edge_tile], rows + 2 * REACH)
            kept = jnp.where(frame_lane % REACH >= 2 * REACH - step_w, found, jnp.zeros_like(found))
            row = edge_pad + (step_w - STEPS + REACH) * frame_rows
            edge_own[row : row + frame_rows] = kept

    def add_edges(owner):
        @pl.when(owner < j)
        def _():
            edge_left[...] = edges[owner].reshape(frame_rows, channels)

        @pl.when(owner > j)
        def _():
            edge_left[...] = -gather_edge(lambda h: others[owner, h, :, :, edge_tile], rows)

        plain = edge_left[...]
        turned_edges = [plain] + [pltpu.roll(plain, REACH * b, axis=1) for b in range(1, STEPS)]
        left = jnp.concatenate(turned_edges, axis=0)
        result = lax.dot_general(
            left, edge_own[...], (((1,), (1,)), ((), ())), preferred_element_type=jnp.float32
        )
        for b in range(STEPS):
            acc[b, :, edge_outs] = acc[b, :, edge_outs] + result[b * frame_rows : (b + 1) * frame_rows]

    def pack(slot):
        def step(step_h, carry):
            moved = {}
            for t in range(frames):
                for g in range(col_count):
                    row = t * block + g * group
                    turn = (g - t) % col_count * block
                    for tile in range(acc.shape[2] // channels):
                        piece = acc[step_h, row : row + group, tile * channels : (tile + 1) * channels]
                        moved[t, g, tile] = pltpu.roll(piece, turn, axis=1) if turn else piece
            for step_w in range(STEPS):
                for step_t in range(STEPS):
                    shift = step_t - REACH
                    base = step_w * frames + shift
                    packed = None
                    for g in range(col_count):
                        total = None
                        for t in range(max(0, -shift), min(frames, frames - shift)):
                            term = moved[t, g, (base + t) // col_count]
                            total = term if total is None else total + term
                        if total is None:
                            total = jnp.zeros((group, channels), jnp.float32)
                        packed = total if packed is None else jnp.where(lane_block == (base + g) % col_count, total, packed)
                    turn = -base % col_count * block
                    packed = pltpu.roll(packed, turn, axis=1) if turn else packed
                    part[slot, step_t * STEPS * STEPS + step_h * STEPS + step_w] = packed
            return carry

        lax.fori_loop(0, STEPS, step, 0)

    def half_slot(owner):
        lanes = pl.ds(pl.multiple_of(jnp.where(owner < j, cut, 0), cut), cut)
        products(lambda h: others[owner, h, :, :, lanes], lanes, cut)
        add_edges(owner)

    turns = [*range(1, half), 0]

    def near_copy(slot, r):
        target = lax.rem(place + r, half)
        return pltpu.make_async_remote_copy(
            src_ref=part.at[slot, pl.ds(first_lag(2 * target + 1 - parity), span)],
            dst_ref=near.at[slot, r],
            send_sem=near_send.at[slot, r],
            recv_sem=near_recv.at[slot, r],
            device_id={"ha": partner},
            device_id_type=MESH,
        )

    def far_copy(slot, r):
        target = lax.rem(place + r, half)
        return pltpu.make_async_remote_copy(
            src_ref=mixed.at[slot, r],
            dst_ref=far.at[slot, r - 1],
            send_sem=far_send.at[slot, r - 1],
            recv_sem=far_recv.at[slot, r - 1],
            device_id={"ha": 2 * target + parity},
            device_id_type=MESH,
        )

    def direct_copy(slot):
        owner = owner_of(slot)
        return pltpu.make_async_remote_copy(
            src_ref=summed.at[slot],
            dst_ref=direct.at[j],
            send_sem=direct_send.at[slot],
            recv_sem=direct_recv.at[j],
            device_id={"col": owner},
            device_id_type=MESH,
        )

    def direct_arrival(owner):
        return pltpu.make_async_remote_copy(
            src_ref=direct.at[owner],
            dst_ref=direct.at[owner],
            send_sem=direct_send.at[0],
            recv_sem=direct_recv.at[owner],
            device_id={"col": owner},
            device_id_type=MESH,
        )

    def turned_copy(slot):
        owner = owner_of(slot)
        return pltpu.make_async_remote_copy(
            src_ref=summed.at[slot],
            dst_ref=turned.at[owner],
            send_sem=turned_send.at[slot],
            recv_sem=turned_recv.at[slot],
            device_id={"ha": mirror},
            device_id_type=MESH,
        )

    def pass_near(slot):
        def action():
            for r in turns:
                near_copy(slot, r).start()

        when_active(slot, action)

    def pass_far(slot):
        def action():
            for r in turns:
                target = lax.rem(place + r, half)
                near_copy(slot, r).wait_recv()
                mixed[slot, r] = part[slot, pl.ds(first_lag(2 * target + parity), span)] + near[slot, r]
                if r > 0:
                    far_copy(slot, r).start()

        when_active(slot, action)

    def finish(slot):
        def action():
            total = mixed[slot, 0]
            for r in range(1, half):
                far_copy(slot, r).wait_recv()
                total = total + far[slot, r - 1]
            if slot == 0:
                direct[j] = total
            else:
                summed[slot] = total
                direct_copy(slot).start()
                turned_copy(slot).start()

        when_active(slot, action)

    if col_count > 1:
        advance(0, spread[3])

    def relay(quarter):
        if col_count > 2:
            advance(1, spread[quarter])

    diagonal(outside)
    pack(0)
    pass_near(0)
    relay(0)
    relay(1)
    gather_own_edges()
    for slot in range(1, col_count):
        owner = owner_of(slot)
        if slot == 1:

            @pl.when(jnp.logical_not(same_side))
            def _():
                half_slot(owner)
                pack(slot)

            pass_near(slot)
            relay(2)
            pass_far(0)
            relay(3)
            pass_far(slot)
            continue
        if slot > 2:

            @pl.when(jnp.logical_not(inner))
            def _():
                pass_far(slot - 1)

            advance(slot - 1, halves)
        if slot == middle + 1:
            for way in range(2):

                @pl.when(receives_rest(way))
                def _():
                    for h in range(rows):
                        arrival(way, rest, h).wait_recv()

        if whole(slot) is None:
            half_slot(owner)
        else:

            @pl.when(whole(slot))
            def _():
                products(lambda h: others[owner, h], pl.ds(0, width), width)

            @pl.when(jnp.logical_not(whole(slot)))
            def _():
                half_slot(owner)

        pack(slot)
        pass_near(slot)
        if slot > 2:

            @pl.when(inner)
            def _():
                pass_far(slot - 1)

            finish(slot - 2)
            if slot == col_count - 1:

                @pl.when(jnp.logical_not(inner))
                def _():
                    finish(slot - 1)

        if slot == 2:
            finish(0)
    if col_count > 2:
        pass_far(col_count - 1)

        @pl.when(inner)
        def _():
            finish(col_count - 2)

    elif col_count > 1:
        finish(0)
    else:
        pass_far(0)
    finish(col_count - 1)

    def assemble(ref, index):
        tiles = [ref[q, index] for q in range(col_count)]
        lines = []
        for g in range(col_count):
            line = None
            for q in range(col_count):
                turn = (q - g) * block % channels
                tile = pltpu.roll(tiles[q], turn, axis=1) if turn else tiles[q]
                line = tile if line is None else jnp.where(lane_block == q, tile, line)
            lines.append(line)
        return lines

    for slot in range(1, col_count):
        owner = owner_of(slot)
        if whole(slot) is None:
            direct_arrival(owner).wait_recv()
        else:
            pl.when(jnp.logical_not(whole(slot)))(lambda: direct_arrival(owner).wait_recv())
        when_active(slot, lambda: turned_copy(slot).wait_recv())

    reach_index = lag_count - 1 - first_lag(i) - first_lag(mirror)
    for base in range(0, span, col_count):
        taken = range(base, min(base + col_count, span))
        lines = []
        for k in taken:
            lines.extend(assemble(turned, jnp.clip(reach_index - k, 0, span - 1)))
        lines.extend([jnp.zeros((group, channels), jnp.float32)] * (channels // group - len(lines)))
        flipped = jnp.concatenate(lines, axis=0).T
        for at, k in enumerate(taken):
            plain = assemble(direct, k)
            for g in range(col_count):
                line = None
                for q in range(col_count):
                    row = q * block + g * group
                    turn = (q - at) * block % channels
                    tile = flipped[row : row + group]
                    tile = pltpu.roll(tile, turn, axis=1) if turn else tile
                    line = tile if line is None else jnp.where(lane_block == q, tile, line)
                out_ref[g * group : (g + 1) * group, k * channels : (k + 1) * channels] = (plain[g] + line) * scale

    def settle(slot):
        def action():
            for r in turns:
                near_copy(slot, r).wait_send()
                if r > 0:
                    far_copy(slot, r).wait_send()
            if slot > 0:
                direct_copy(slot).wait_send()
                turned_copy(slot).wait_send()

        when_active(slot, action)

    for slot in range(col_count):
        settle(slot)
    for way in range(2):
        for step in range(col_count - 1):

            @pl.when(sends(way, step))
            def _():
                for h in range(rows):
                    hop(way, step, h).wait_send()

        @pl.when(sends_rest(way))
        def _():
            for h in range(rows):
                hop(way, rest, h).wait_send()

    for step in range(col_count - 1):

        @pl.when(sends(0, step))
        def _():
            edge_hop(step).wait_send()

    for way, has in ((0, has_after), (1, has_before)):

        @pl.when(has)
        def _():
            for r in range(REACH):
                halo(way, r).wait_send()


def body(ha_count, col_count, features):
    frames, rows, block, width = features.shape
    channels = block * col_count
    lag_count = STEPS**3
    share, span = window_plan(lag_count, channels, ha_count)
    half = ha_count // 2
    group = block // col_count
    dma = pltpu.SemaphoreType.DMA
    lines = max(col_count - 1, 1)
    lanes = -(-STEPS * frames * block // channels) * channels
    tiles = pltpu.VMEM((col_count, span, group, channels), jnp.float32)
    edge_first = (STEPS - REACH) * frames * block // channels * channels
    window = pl.pallas_call(
        functools.partial(kernel, ha_count, col_count),
        out_shape=pltpu.VMEM((block, span * channels), jnp.float32),
        in_specs=[pl.BlockSpec(memory_space=pl.ANY)],
        out_specs=pl.BlockSpec(memory_space=pltpu.VMEM),
        scratch_shapes=[
            pltpu.VMEM((rows + 2 * REACH, STEPS, frames, block, width), features.dtype),
            pltpu.VMEM((col_count, rows, frames, block, width), features.dtype),
            pltpu.VMEM((STEPS, frames * block, lanes), jnp.float32),
            pltpu.VMEM((col_count, lag_count, group, channels), jnp.float32),
            pltpu.VMEM((col_count, half, span, group, channels), jnp.float32),
            pltpu.VMEM((col_count, half, span, group, channels), jnp.float32),
            pltpu.VMEM((col_count, half, span, group, channels), jnp.float32),
            tiles,
            tiles,
            tiles,
            pltpu.VMEM((col_count, frames, block, channels), features.dtype),
            pltpu.VMEM((frames * block, channels), features.dtype),
            pltpu.VMEM((STEPS * frames * block - edge_first, channels), features.dtype),
            dma((rows,)),
            dma((2, REACH)),
            dma((2, REACH)),
            dma((2, lines + 1, rows)),
            dma((2, lines + 1, rows)),
            dma((col_count, half)),
            dma((col_count, half)),
            dma((col_count, half)),
            dma((col_count, half)),
            dma((col_count,)),
            dma((col_count,)),
            dma((col_count,)),
            dma((col_count,)),
            dma((lines,)),
            dma((lines,)),
        ],
        compiler_params=pltpu.CompilerParams(collective_id=0, has_side_effects=True),
        name="lag_cov",
    )(features)
    i = lax.axis_index("ha")
    first = jnp.minimum(i * share // channels, lag_count - span)
    return lax.dynamic_slice_in_dim(window, i * share - first * channels, share, 1)


def solution(mesh):
    in_specs = (P(None, "ha", "col", None),)
    out_specs = P("col", "ha")
    counts = (mesh.shape["ha"], mesh.shape["col"])
    return jax.shard_map(
        functools.partial(body, *counts), mesh=mesh, in_specs=in_specs, out_specs=out_specs, check_vma=False
    )
```

```python
import functools

import jax
import jax.numpy as jnp
from jax import lax
from jax.experimental import pallas as pl
from jax.experimental.pallas import tpu as pltpu
from jax.sharding import PartitionSpec as P

MESH = pl.DeviceIdType.MESH
REACH = 2
STEPS = 2 * REACH + 1


def window_plan(lag_count, channels, ha_count):
    share = lag_count * channels // ha_count
    spans = [-(-(i + 1) * share // channels) - i * share // channels for i in range(ha_count)]
    return share, max(spans)


def kernel(
    ha_count, col_count, x_ref, out_ref, stack, others, acc, part, near, mixed, far, summed, direct, turned,
    edges, edge_left, edge_own,
    local_sem, halo_send, halo_recv, line_send, line_recv, near_send, near_recv, far_send, far_recv,
    direct_send, direct_recv, turned_send, turned_recv, edge_send, edge_recv,
):
    frames, rows, block, width = x_ref.shape
    channels = block * col_count
    lag_count = STEPS**3
    share, span = window_plan(lag_count, channels, ha_count)
    i, j = lax.axis_index("ha"), lax.axis_index("col")
    half = ha_count // 2
    parity, place = lax.rem(i, 2), lax.div(i, 2)
    partner = i + 1 - 2 * parity
    mirror = ha_count - 1 - i
    pieces = [pl.ds(0, -(-span // 2)), pl.ds(-(-span // 2), span // 2)][: min(span, 2)]
    middle = col_count // 2
    cut = width // 2
    frame_rows = frames * block

    def first_lag(index):
        return jnp.minimum(lax.div(index * share, channels), lag_count - span)

    barrier = pltpu.get_barrier_semaphore()
    for step in range(1, ha_count):
        pl.semaphore_signal(
            barrier, inc=1, device_id={"ha": lax.rem(i + step, ha_count)}, device_id_type=MESH
        )

    @pl.when(j > 0)
    def _():
        pl.semaphore_signal(barrier, inc=1, device_id={"col": j - 1}, device_id_type=MESH)

    @pl.when(j < col_count - 1)
    def _():
        pl.semaphore_signal(barrier, inc=1, device_id={"col": j + 1}, device_id_type=MESH)

    own_copies = [
        pltpu.make_async_copy(x_ref.at[:, h], stack.at[REACH + h, REACH], local_sem.at[h])
        for h in range(rows)
    ]
    for copy in own_copies:
        copy.start()

    ends = (j > 0).astype(jnp.int32) + (j < col_count - 1).astype(jnp.int32)
    pl.semaphore_wait(barrier, ha_count - 1 + ends)

    def halo(way, r):
        source = rows - REACH + r if way == 0 else r
        slot = r if way == 0 else rows + REACH + r
        return pltpu.make_async_remote_copy(
            src_ref=x_ref.at[:, source],
            dst_ref=stack.at[slot, REACH],
            send_sem=halo_send.at[way, r],
            recv_sem=halo_recv.at[way, r],
            device_id={"ha": (i + 1) if way == 0 else (i - 1)},
            device_id_type=MESH,
        )

    rest = max(col_count - 1, 1)

    def lanes_of(way):
        return pl.ds(cut, cut) if way == 0 else pl.ds(0, cut)

    def hop(way, step, h):
        sign = 1 if way == 0 else -1
        fresh = step in (0, rest)
        owner = j if fresh else j - sign * step
        lanes = lanes_of(1 - way if step == rest else way)
        return pltpu.make_async_remote_copy(
            src_ref=x_ref.at[:, h, :, lanes] if fresh else others.at[owner, h, :, :, lanes],
            dst_ref=others.at[owner, h, :, :, lanes],
            send_sem=line_send.at[way, step, h],
            recv_sem=line_recv.at[way, step, h],
            device_id={"col": j + sign},
            device_id_type=MESH,
        )

    def edge_hop(step):
        return pltpu.make_async_remote_copy(
            src_ref=edges.at[j - step],
            dst_ref=edges.at[j - step],
            send_sem=edge_send.at[step],
            recv_sem=edge_recv.at[step],
            device_id={"col": j + 1},
            device_id_type=MESH,
        )

    def edge_arrival(step):
        owner = j - 1 - step
        return pltpu.make_async_remote_copy(
            src_ref=edges.at[owner],
            dst_ref=edges.at[owner],
            send_sem=edge_send.at[step],
            recv_sem=edge_recv.at[step],
            device_id={"col": j - 1},
            device_id_type=MESH,
        )

    def travels(way, owner):
        if way == 0:
            useful = True if col_count - 2 < middle else owner != col_count - 2
            return jnp.logical_and(owner >= 0, useful)
        useful = True if 1 >= middle else owner != 1
        return jnp.logical_and(owner <= col_count - 1, useful)

    def sends(way, step):
        if way == 0:
            return jnp.logical_and(j < col_count - 1, travels(0, j - step))
        return jnp.logical_and(j > 0, travels(1, j + step))

    def receives(way, step):
        return travels(0, j - 1 - step) if way == 0 else travels(1, j + 1 + step)

    def sends_rest(way):
        return j + 1 < middle if way == 0 else j - 1 >= middle

    def receives_rest(way):
        if way == 0:
            return jnp.logical_and(j >= 1, j < middle)
        return jnp.logical_and(j >= middle, j < col_count - 1)

    def arrival(way, step, h):
        sign = 1 if way == 0 else -1
        owner = j - sign * (1 if step == rest else step + 1)
        lanes = lanes_of(1 - way if step == rest else way)
        return pltpu.make_async_remote_copy(
            src_ref=others.at[owner, h, :, :, lanes],
            dst_ref=others.at[owner, h, :, :, lanes],
            send_sem=line_send.at[way, step, h],
            recv_sem=line_recv.at[way, step, h],
            device_id={"col": j - sign},
            device_id_type=MESH,
        )

    for way in range(2):

        @pl.when(sends(way, 0))
        def _():
            for h in range(rows):
                hop(way, 0, h).start()

    has_after, has_before = i < ha_count - 1, i > 0
    for way, has in ((0, has_after), (1, has_before)):

        @pl.when(has)
        def _():
            for r in range(REACH):
                halo(way, r).start()

    inner = jnp.minimum(j, col_count - 1 - j) >= 1
    low = j < middle
    same_side = jnp.where(low, j + 1 < middle, j - 1 >= middle)
    inward = jnp.where(low, 1, -1)
    both = jnp.minimum(j, col_count - 1 - j)

    def owner_of(slot):
        inwards = col_count - 1 - both
        return jnp.where(slot <= inwards, j + inward * slot, j - inward * (slot - inwards))

    def whole(slot):
        if 1 <= col_count - slot < middle:
            return both == col_count - slot
        return None

    def when_active(slot, action):
        if slot == 1:
            pl.when(jnp.logical_not(same_side))(action)
        else:
            action()

    blank = jnp.zeros(direct.shape[1:], direct.dtype)
    turned[j] = blank
    if col_count > 1:

        @pl.when(same_side)
        def _():
            turned[j + inward] = blank

    @pl.when(inner)
    def _():
        direct[j - inward] = blank

    frame_lane = lax.broadcasted_iota(jnp.int32, (frame_rows, channels), 1)

    def shift_rows(first, count):
        def step(index, carry):
            row = first + index
            plain = stack[row, REACH].reshape(frame_rows, width)
            for step_w in range(STEPS):
                shift = REACH - step_w
                if shift != 0:
                    moved = pltpu.roll(plain, shift % width, axis=1)
                    if shift > 0:
                        head = moved[:, :channels]
                        head = jnp.where(frame_lane >= shift, head, jnp.zeros_like(head))
                        moved = jnp.concatenate([head, moved[:, channels:]], axis=1)
                    else:
                        tail = moved[:, width - channels :]
                        tail = jnp.where(frame_lane < channels + shift, tail, jnp.zeros_like(tail))
                        moved = jnp.concatenate([moved[:, : width - channels], tail], axis=1)
                    stack[row, step_w] = moved.reshape(frames, block, width)
            return carry

        lax.fori_loop(0, count, step, 0)

    for copy in own_copies:
        copy.wait()

    edge_tile = pl.ds(cut - channels, channels)

    def gather_edge(field, count):
        total = jnp.zeros((frame_rows, channels), stack.dtype)
        for h in range(count):
            tile = field(h).reshape(frame_rows, channels)
            moved = pltpu.roll(tile, (REACH * (h + 1)) % channels, axis=1)
            total = jnp.where(frame_lane // REACH == h, moved, total)
        return total

    @pl.when(sends(0, 0))
    def _():
        own_edge = gather_edge(lambda h: stack[REACH + h, REACH, :, :, edge_tile], rows)
        edges[j] = own_edge.reshape(frames, block, channels)
        edge_hop(0).start()

    for way in range(2):

        @pl.when(sends_rest(way))
        def _():
            for h in range(rows):
                hop(way, rest, h).start()

    shift_rows(REACH, rows)

    def advance(step, part_rows):
        for h in part_rows:
            for way in range(2):

                @pl.when(receives(way, step))
                def _():
                    arrival(way, step, h).wait_recv()

                if step + 1 < col_count - 1:

                    @pl.when(sends(way, step + 1))
                    def _():
                        hop(way, step + 1, h).start()

        if rows - 1 in part_rows:

            @pl.when(receives(0, step))
            def _():
                edge_arrival(step).wait_recv()

            if step + 1 < col_count - 1:

                @pl.when(sends(0, step + 1))
                def _():
                    edge_hop(step + 1).start()

    halves = list(range(rows))
    def products(field, lanes, depth, places=None, seen=None):
        seen = set() if seen is None else seen
        for r in range(rows + 2 * REACH) if places is None else places:
            picked = range(max(0, r - 2 * REACH), min(rows - 1, r) + 1)
            left = jnp.concatenate([field(h).reshape(frame_rows, depth) for h in picked], axis=0)
            own = stack[r, :, :, :, lanes].reshape(STEPS * frame_rows, depth)
            result = lax.dot_general(
                left, own, (((1,), (1,)), ((), ())), preferred_element_type=jnp.float32
            )
            for place_in, h in enumerate(picked):
                piece = result[place_in * frame_rows : (place_in + 1) * frame_rows]
                outs = pl.ds(0, STEPS * frame_rows)
                if r - h in seen:
                    acc[r - h, :, outs] = acc[r - h, :, outs] + piece
                else:
                    acc[r - h, :, outs] = piece
                    seen.add(r - h)

    diagonal_seen = set()

    def diagonal(places):
        products(lambda h: stack[REACH + h, REACH], pl.ds(0, width), width, places, diagonal_seen)

    inside = list(range(REACH, REACH + rows))
    outside = [*range(REACH), *range(REACH + rows, rows + 2 * REACH)]
    spread = [halves[n * rows // 4 : (n + 1) * rows // 4] for n in range(4)]
    for quarter in range(3):
        if col_count > 1:
            advance(0, spread[quarter])
        if quarter < 2:
            diagonal(inside[quarter * rows // 2 : (quarter + 1) * rows // 2])

    for way, has_in, place_row in ((0, has_before, 0), (1, has_after, rows + REACH)):

        @pl.when(has_in)
        def _():
            for r in range(REACH):
                halo(way, r).wait_recv()
            shift_rows(place_row, REACH)

        @pl.when(jnp.logical_not(has_in))
        def _():
            for r in range(REACH):
                stack[place_row + r] = jnp.zeros(stack.shape[1:], stack.dtype)

    group = block // col_count
    scale = 1.0 / (frames * rows * ha_count * width)
    lane_block = lax.broadcasted_iota(jnp.int32, (group, channels), 1) // block

    edge_first = (STEPS - REACH) * frame_rows // channels * channels
    edge_pad = (STEPS - REACH) * frame_rows - edge_first
    edge_outs = pl.ds(edge_first, STEPS * frame_rows - edge_first)

    def gather_own_edges():
        if edge_pad:
            edge_own[:edge_pad] = jnp.zeros((edge_pad, channels), edge_own.dtype)
        for step_w in range(STEPS - REACH, STEPS):
            found = gather_edge(lambda r: stack[r, step_w, :, :, edge_tile], rows + 2 * REACH)
            kept = jnp.where(frame_lane % REACH >= 2 * REACH - step_w, found, jnp.zeros_like(found))
            row = edge_pad + (step_w - STEPS + REACH) * frame_rows
            edge_own[row : row + frame_rows] = kept

    def add_edges(owner):
        @pl.when(owner < j)
        def _():
            edge_left[...] = edges[owner].reshape(frame_rows, channels)

        @pl.when(owner > j)
        def _():
            edge_left[...] = -gather_edge(lambda h: others[owner, h, :, :, edge_tile], rows)

        plain = edge_left[...]
        turned_edges = [plain] + [pltpu.roll(plain, REACH * b, axis=1) for b in range(1, STEPS)]
        left = jnp.concatenate(turned_edges, axis=0)
        result = lax.dot_general(
            left, edge_own[...], (((1,), (1,)), ((), ())), preferred_element_type=jnp.float32
        )
        for b in range(STEPS):
            acc[b, :, edge_outs] = acc[b, :, edge_outs] + result[b * frame_rows : (b + 1) * frame_rows]

    def pack(slot):
        def step(step_h, carry):
            moved = {}
            for t in range(frames):
                for g in range(col_count):
                    row = t * block + g * group
                    turn = (g - t) % col_count * block
                    for tile in range(acc.shape[2] // channels):
                        piece = acc[step_h, row : row + group, tile * channels : (tile + 1) * channels]
                        moved[t, g, tile] = pltpu.roll(piece, turn, axis=1) if turn else piece
            for step_w in range(STEPS):
                for step_t in range(STEPS):
                    shift = step_t - REACH
                    base = step_w * frames + shift
                    packed = None
                    for g in range(col_count):
                        total = None
                        for t in range(max(0, -shift), min(frames, frames - shift)):
                            term = moved[t, g, (base + t) // col_count]
                            total = term if total is None else total + term
                        if total is None:
                            total = jnp.zeros((group, channels), jnp.float32)
                        packed = total if packed is None else jnp.where(lane_block == (base + g) % col_count, total, packed)
                    turn = -base % col_count * block
                    packed = pltpu.roll(packed, turn, axis=1) if turn else packed
                    part[slot, step_t * STEPS * STEPS + step_h * STEPS + step_w] = packed
            return carry

        lax.fori_loop(0, STEPS, step, 0, unroll=True)

    def half_slot(owner):
        lanes = pl.ds(pl.multiple_of(jnp.where(owner < j, cut, 0), cut), cut)
        products(lambda h: others[owner, h, :, :, lanes], lanes, cut)
        add_edges(owner)

    turns = [*range(1, half), 0]

    def near_copy(slot, r):
        target = lax.rem(place + r, half)
        return pltpu.make_async_remote_copy(
            src_ref=part.at[slot, pl.ds(first_lag(2 * target + 1 - parity), span)],
            dst_ref=near.at[slot, r],
            send_sem=near_send.at[slot, r],
            recv_sem=near_recv.at[slot, r],
            device_id={"ha": partner},
            device_id_type=MESH,
        )

    def far_copy(slot, r, c):
        target = lax.rem(place + r, half)
        return pltpu.make_async_remote_copy(
            src_ref=mixed.at[slot, r, pieces[c]],
            dst_ref=far.at[slot, r - 1, pieces[c]],
            send_sem=far_send.at[slot, r - 1, c],
            recv_sem=far_recv.at[slot, r - 1, c],
            device_id={"ha": 2 * target + parity},
            device_id_type=MESH,
        )

    def direct_copy(slot, c):
        owner = owner_of(slot)
        return pltpu.make_async_remote_copy(
            src_ref=summed.at[slot, pieces[c]],
            dst_ref=direct.at[j, pieces[c]],
            send_sem=direct_send.at[slot, c],
            recv_sem=direct_recv.at[j, c],
            device_id={"col": owner},
            device_id_type=MESH,
        )

    def direct_arrival(owner, c):
        return pltpu.make_async_remote_copy(
            src_ref=direct.at[owner, pieces[c]],
            dst_ref=direct.at[owner, pieces[c]],
            send_sem=direct_send.at[0, c],
            recv_sem=direct_recv.at[owner, c],
            device_id={"col": owner},
            device_id_type=MESH,
        )

    def turned_copy(slot, c):
        owner = owner_of(slot)
        return pltpu.make_async_remote_copy(
            src_ref=summed.at[slot, pieces[c]],
            dst_ref=turned.at[owner, pieces[c]],
            send_sem=turned_send.at[slot, c],
            recv_sem=turned_recv.at[slot, c],
            device_id={"ha": mirror},
            device_id_type=MESH,
        )

    def pass_near(slot):
        def action():
            for r in turns:
                near_copy(slot, r).start()

        when_active(slot, action)

    def pass_far(slot):
        def action():
            for r in turns:
                target = lax.rem(place + r, half)
                near_copy(slot, r).wait_recv()
                mixed[slot, r] = part[slot, pl.ds(first_lag(2 * target + parity), span)] + near[slot, r]
                if r > 0:
                    far_copy(slot, r, 0).start()
            for c in range(1, len(pieces)):
                for r in range(1, half):
                    far_copy(slot, r, c).start()

        when_active(slot, action)

    def finish(slot):
        def action():
            for c, piece in enumerate(pieces):
                total = mixed[slot, 0, piece]
                for r in range(1, half):
                    far_copy(slot, r, c).wait_recv()
                    total = total + far[slot, r - 1, piece]
                if slot == 0:
                    direct[j, piece] = total
                else:
                    summed[slot, piece] = total
                    direct_copy(slot, c).start()
                    turned_copy(slot, c).start()

        when_active(slot, action)

    if col_count > 1:
        advance(0, spread[3])

    def relay(quarter):
        if col_count > 2:
            advance(1, spread[quarter])

    diagonal(outside)
    pack(0)
    pass_near(0)
    relay(0)
    relay(1)
    gather_own_edges()
    pass_far(0)
    for slot in range(1, col_count):
        owner = owner_of(slot)
        if slot == 1:

            @pl.when(jnp.logical_not(same_side))
            def _():
                half_slot(owner)
                pack(slot)

            pass_near(slot)
            relay(2)
            relay(3)
            pass_far(slot)
            continue
        if slot > 2:

            @pl.when(jnp.logical_not(inner))
            def _():
                pass_far(slot - 1)

            advance(slot - 1, halves)
        if slot == middle + 1:
            for way in range(2):

                @pl.when(receives_rest(way))
                def _():
                    for h in range(rows):
                        arrival(way, rest, h).wait_recv()

        if whole(slot) is None:
            half_slot(owner)
        else:

            @pl.when(whole(slot))
            def _():
                products(lambda h: others[owner, h], pl.ds(0, width), width)

            @pl.when(jnp.logical_not(whole(slot)))
            def _():
                half_slot(owner)

        if slot > 2:

            @pl.when(inner)
            def _():
                pass_far(slot - 1)
                finish(slot - 2)

        pack(slot)
        pass_near(slot)
        if slot > 2:

            @pl.when(jnp.logical_not(inner))
            def _():
                finish(slot - 2)

            if slot == col_count - 1:

                @pl.when(jnp.logical_not(inner))
                def _():
                    finish(slot - 1)

    if col_count > 2:
        pass_far(col_count - 1)

        @pl.when(inner)
        def _():
            finish(col_count - 2)

    elif col_count > 1:
        finish(0)
    else:
        pass_far(0)
    finish(0)
    finish(col_count - 1)

    def assemble(ref, index):
        tiles = [ref[q, index] for q in range(col_count)]
        lines = []
        for g in range(col_count):
            line = None
            for q in range(col_count):
                turn = (q - g) * block % channels
                tile = pltpu.roll(tiles[q], turn, axis=1) if turn else tiles[q]
                line = tile if line is None else jnp.where(lane_block == q, tile, line)
            lines.append(line)
        return lines

    for slot in range(1, col_count):
        owner = owner_of(slot)
        for c in range(len(pieces)):
            if whole(slot) is None:
                direct_arrival(owner, c).wait_recv()
            else:
                pl.when(jnp.logical_not(whole(slot)))(lambda: direct_arrival(owner, c).wait_recv())
            when_active(slot, lambda: turned_copy(slot, c).wait_recv())

    reach_index = lag_count - 1 - first_lag(i) - first_lag(mirror)
    for base in range(0, span, col_count):
        taken = range(base, min(base + col_count, span))
        lines = []
        for k in taken:
            lines.extend(assemble(turned, jnp.clip(reach_index - k, 0, span - 1)))
        lines.extend([jnp.zeros((group, channels), jnp.float32)] * (channels // group - len(lines)))
        flipped = jnp.concatenate(lines, axis=0).T
        for at, k in enumerate(taken):
            plain = assemble(direct, k)
            for g in range(col_count):
                line = None
                for q in range(col_count):
                    row = q * block + g * group
                    turn = (q - at) * block % channels
                    tile = flipped[row : row + group]
                    tile = pltpu.roll(tile, turn, axis=1) if turn else tile
                    line = tile if line is None else jnp.where(lane_block == q, tile, line)
                out_ref[g * group : (g + 1) * group, k * channels : (k + 1) * channels] = (plain[g] + line) * scale

    def settle(slot):
        def action():
            for r in turns:
                near_copy(slot, r).wait_send()
                for c in range(len(pieces)):
                    if r > 0:
                        far_copy(slot, r, c).wait_send()
            for c in range(len(pieces)):
                if slot > 0:
                    direct_copy(slot, c).wait_send()
                    turned_copy(slot, c).wait_send()

        when_active(slot, action)

    for slot in range(col_count):
        settle(slot)
    for way in range(2):
        for step in range(col_count - 1):

            @pl.when(sends(way, step))
            def _():
                for h in range(rows):
                    hop(way, step, h).wait_send()

        @pl.when(sends_rest(way))
        def _():
            for h in range(rows):
                hop(way, rest, h).wait_send()

    for step in range(col_count - 1):

        @pl.when(sends(0, step))
        def _():
            edge_hop(step).wait_send()

    for way, has in ((0, has_after), (1, has_before)):

        @pl.when(has)
        def _():
            for r in range(REACH):
                halo(way, r).wait_send()


def body(ha_count, col_count, features):
    frames, rows, block, width = features.shape
    channels = block * col_count
    lag_count = STEPS**3
    share, span = window_plan(lag_count, channels, ha_count)
    half = ha_count // 2
    group = block // col_count
    dma = pltpu.SemaphoreType.DMA
    lines = max(col_count - 1, 1)
    lanes = -(-STEPS * frames * block // channels) * channels
    tiles = pltpu.VMEM((col_count, span, group, channels), jnp.float32)
    edge_first = (STEPS - REACH) * frames * block // channels * channels
    window = pl.pallas_call(
        functools.partial(kernel, ha_count, col_count),
        out_shape=pltpu.VMEM((block, span * channels), jnp.float32),
        in_specs=[pl.BlockSpec(memory_space=pl.ANY)],
        out_specs=pl.BlockSpec(memory_space=pltpu.VMEM),
        scratch_shapes=[
            pltpu.VMEM((rows + 2 * REACH, STEPS, frames, block, width), features.dtype),
            pltpu.VMEM((col_count, rows, frames, block, width), features.dtype),
            pltpu.VMEM((STEPS, frames * block, lanes), jnp.float32),
            pltpu.VMEM((col_count, lag_count, group, channels), jnp.float32),
            pltpu.VMEM((col_count, half, span, group, channels), jnp.float32),
            pltpu.VMEM((col_count, half, span, group, channels), jnp.float32),
            pltpu.VMEM((col_count, half, span, group, channels), jnp.float32),
            tiles,
            tiles,
            tiles,
            pltpu.VMEM((col_count, frames, block, channels), features.dtype),
            pltpu.VMEM((frames * block, channels), features.dtype),
            pltpu.VMEM((STEPS * frames * block - edge_first, channels), features.dtype),
            dma((rows,)),
            dma((2, REACH)),
            dma((2, REACH)),
            dma((2, lines + 1, rows)),
            dma((2, lines + 1, rows)),
            dma((col_count, half)),
            dma((col_count, half)),
            dma((col_count, half, 2)),
            dma((col_count, half, 2)),
            dma((col_count, 2)),
            dma((col_count, 2)),
            dma((col_count, 2)),
            dma((col_count, 2)),
            dma((lines,)),
            dma((lines,)),
        ],
        compiler_params=pltpu.CompilerParams(collective_id=0, has_side_effects=True),
        name="lag_cov",
    )(features)
    i = lax.axis_index("ha")
    first = jnp.minimum(i * share // channels, lag_count - span)
    return lax.dynamic_slice_in_dim(window, i * share - first * channels, share, 1)


def solution(mesh):
    in_specs = (P(None, "ha", "col", None),)
    out_specs = P("col", "ha")
    counts = (mesh.shape["ha"], mesh.shape["col"])
    return jax.shard_map(
        functools.partial(body, *counts), mesh=mesh, in_specs=in_specs, out_specs=out_specs, check_vma=False
    )
```

```python
import functools

import jax
import jax.numpy as jnp
from jax import lax
from jax.experimental import pallas as pl
from jax.experimental.pallas import tpu as pltpu
from jax.sharding import PartitionSpec as P

MESH = pl.DeviceIdType.MESH
REACH = 2
STEPS = 2 * REACH + 1


def window_plan(lag_count, channels, ha_count):
    share = lag_count * channels // ha_count
    spans = [-(-(i + 1) * share // channels) - i * share // channels for i in range(ha_count)]
    return share, max(spans)


def kernel(
    ha_count, col_count, x_ref, out_ref, stack, others, acc, part, near, mixed, far, summed, direct, turned,
    edges, edge_left, edge_own,
    local_sem, halo_send, halo_recv, line_send, line_recv, near_send, near_recv, far_send, far_recv,
    direct_send, direct_recv, turned_send, turned_recv, edge_send, edge_recv,
):
    frames, rows, block, width = x_ref.shape
    channels = block * col_count
    lag_count = STEPS**3
    share, span = window_plan(lag_count, channels, ha_count)
    i, j = lax.axis_index("ha"), lax.axis_index("col")
    half = ha_count // 2
    parity, place = lax.rem(i, 2), lax.div(i, 2)
    partner = i + 1 - 2 * parity
    mirror = ha_count - 1 - i
    pieces = [pl.ds(0, -(-span // 2)), pl.ds(-(-span // 2), span // 2)][: min(span, 2)]
    middle = col_count // 2
    cut = width // 2
    frame_rows = frames * block

    def first_lag(index):
        return jnp.minimum(lax.div(index * share, channels), lag_count - span)

    barrier = pltpu.get_barrier_semaphore()
    for step in range(1, ha_count):
        pl.semaphore_signal(
            barrier, inc=1, device_id={"ha": lax.rem(i + step, ha_count)}, device_id_type=MESH
        )

    @pl.when(j > 0)
    def _():
        pl.semaphore_signal(barrier, inc=1, device_id={"col": j - 1}, device_id_type=MESH)

    @pl.when(j < col_count - 1)
    def _():
        pl.semaphore_signal(barrier, inc=1, device_id={"col": j + 1}, device_id_type=MESH)

    own_copies = [
        pltpu.make_async_copy(x_ref.at[:, h], stack.at[REACH + h, REACH], local_sem.at[h])
        for h in range(rows)
    ]
    for copy in own_copies:
        copy.start()

    ends = (j > 0).astype(jnp.int32) + (j < col_count - 1).astype(jnp.int32)
    pl.semaphore_wait(barrier, ha_count - 1 + ends)

    def halo(way, r):
        source = rows - REACH + r if way == 0 else r
        slot = r if way == 0 else rows + REACH + r
        return pltpu.make_async_remote_copy(
            src_ref=x_ref.at[:, source],
            dst_ref=stack.at[slot, REACH],
            send_sem=halo_send.at[way, r],
            recv_sem=halo_recv.at[way, r],
            device_id={"ha": (i + 1) if way == 0 else (i - 1)},
            device_id_type=MESH,
        )

    rest = max(col_count - 1, 1)

    def lanes_of(way):
        return pl.ds(cut, cut) if way == 0 else pl.ds(0, cut)

    def hop(way, step, h):
        sign = 1 if way == 0 else -1
        fresh = step in (0, rest)
        owner = j if fresh else j - sign * step
        lanes = lanes_of(1 - way if step == rest else way)
        return pltpu.make_async_remote_copy(
            src_ref=x_ref.at[:, h, :, lanes] if fresh else others.at[owner, h, :, :, lanes],
            dst_ref=others.at[owner, h, :, :, lanes],
            send_sem=line_send.at[way, step, h],
            recv_sem=line_recv.at[way, step, h],
            device_id={"col": j + sign},
            device_id_type=MESH,
        )

    def edge_hop(step):
        return pltpu.make_async_remote_copy(
            src_ref=edges.at[j - step],
            dst_ref=edges.at[j - step],
            send_sem=edge_send.at[step],
            recv_sem=edge_recv.at[step],
            device_id={"col": j + 1},
            device_id_type=MESH,
        )

    def edge_arrival(step):
        owner = j - 1 - step
        return pltpu.make_async_remote_copy(
            src_ref=edges.at[owner],
            dst_ref=edges.at[owner],
            send_sem=edge_send.at[step],
            recv_sem=edge_recv.at[step],
            device_id={"col": j - 1},
            device_id_type=MESH,
        )

    def travels(way, owner):
        if way == 0:
            useful = True if col_count - 2 < middle else owner != col_count - 2
            return jnp.logical_and(owner >= 0, useful)
        useful = True if 1 >= middle else owner != 1
        return jnp.logical_and(owner <= col_count - 1, useful)

    def sends(way, step):
        if way == 0:
            return jnp.logical_and(j < col_count - 1, travels(0, j - step))
        return jnp.logical_and(j > 0, travels(1, j + step))

    def receives(way, step):
        return travels(0, j - 1 - step) if way == 0 else travels(1, j + 1 + step)

    def sends_rest(way):
        return j + 1 < middle if way == 0 else j - 1 >= middle

    def receives_rest(way):
        if way == 0:
            return jnp.logical_and(j >= 1, j < middle)
        return jnp.logical_and(j >= middle, j < col_count - 1)

    def arrival(way, step, h):
        sign = 1 if way == 0 else -1
        owner = j - sign * (1 if step == rest else step + 1)
        lanes = lanes_of(1 - way if step == rest else way)
        return pltpu.make_async_remote_copy(
            src_ref=others.at[owner, h, :, :, lanes],
            dst_ref=others.at[owner, h, :, :, lanes],
            send_sem=line_send.at[way, step, h],
            recv_sem=line_recv.at[way, step, h],
            device_id={"col": j - sign},
            device_id_type=MESH,
        )

    for way in range(2):

        @pl.when(sends(way, 0))
        def _():
            for h in range(rows):
                hop(way, 0, h).start()

    has_after, has_before = i < ha_count - 1, i > 0
    for way, has in ((0, has_after), (1, has_before)):

        @pl.when(has)
        def _():
            for r in range(REACH):
                halo(way, r).start()

    inner = jnp.minimum(j, col_count - 1 - j) >= 1
    low = j < middle
    same_side = jnp.where(low, j + 1 < middle, j - 1 >= middle)
    inward = jnp.where(low, 1, -1)
    both = jnp.minimum(j, col_count - 1 - j)

    def owner_of(slot):
        inwards = col_count - 1 - both
        return jnp.where(slot <= inwards, j + inward * slot, j - inward * (slot - inwards))

    def whole(slot):
        if 1 <= col_count - slot < middle:
            return both == col_count - slot
        return None

    def when_active(slot, action):
        if slot == 1:
            pl.when(jnp.logical_not(same_side))(action)
        else:
            action()

    blank = jnp.zeros(direct.shape[1:], direct.dtype)
    turned[j] = blank
    if col_count > 1:

        @pl.when(same_side)
        def _():
            turned[j + inward] = blank

    @pl.when(inner)
    def _():
        direct[j - inward] = blank

    frame_lane = lax.broadcasted_iota(jnp.int32, (frame_rows, channels), 1)

    def shift_rows(first, count):
        def step(index, carry):
            row = first + index
            plain = stack[row, REACH].reshape(frame_rows, width)
            for step_w in range(STEPS):
                shift = REACH - step_w
                if shift != 0:
                    moved = pltpu.roll(plain, shift % width, axis=1)
                    if shift > 0:
                        head = moved[:, :channels]
                        head = jnp.where(frame_lane >= shift, head, jnp.zeros_like(head))
                        moved = jnp.concatenate([head, moved[:, channels:]], axis=1)
                    else:
                        tail = moved[:, width - channels :]
                        tail = jnp.where(frame_lane < channels + shift, tail, jnp.zeros_like(tail))
                        moved = jnp.concatenate([moved[:, : width - channels], tail], axis=1)
                    stack[row, step_w] = moved.reshape(frames, block, width)
            return carry

        lax.fori_loop(0, count, step, 0)

    for copy in own_copies:
        copy.wait()

    edge_tile = pl.ds(cut - channels, channels)

    def gather_edge(field, count):
        total = jnp.zeros((frame_rows, channels), stack.dtype)
        for h in range(count):
            tile = field(h).reshape(frame_rows, channels)
            moved = pltpu.roll(tile, (REACH * (h + 1)) % channels, axis=1)
            total = jnp.where(frame_lane // REACH == h, moved, total)
        return total

    @pl.when(sends(0, 0))
    def _():
        own_edge = gather_edge(lambda h: stack[REACH + h, REACH, :, :, edge_tile], rows)
        edges[j] = own_edge.reshape(frames, block, channels)
        edge_hop(0).start()

    for way in range(2):

        @pl.when(sends_rest(way))
        def _():
            for h in range(rows):
                hop(way, rest, h).start()

    shift_rows(REACH, rows)

    def advance(step, part_rows):
        for h in part_rows:
            for way in range(2):

                @pl.when(receives(way, step))
                def _():
                    arrival(way, step, h).wait_recv()

                if step + 1 < col_count - 1:

                    @pl.when(sends(way, step + 1))
                    def _():
                        hop(way, step + 1, h).start()

        if rows - 1 in part_rows:

            @pl.when(receives(0, step))
            def _():
                edge_arrival(step).wait_recv()

            if step + 1 < col_count - 1:

                @pl.when(sends(0, step + 1))
                def _():
                    edge_hop(step + 1).start()

    halves = list(range(rows))
    def products(field, lanes, depth, places=None, seen=None):
        seen = set() if seen is None else seen
        for r in range(rows + 2 * REACH) if places is None else places:
            picked = range(max(0, r - 2 * REACH), min(rows - 1, r) + 1)
            left = jnp.concatenate([field(h).reshape(frame_rows, depth) for h in picked], axis=0)
            own = stack[r, :, :, :, lanes].reshape(STEPS * frame_rows, depth)
            result = lax.dot_general(
                left, own, (((1,), (1,)), ((), ())), preferred_element_type=jnp.float32
            )
            for place_in, h in enumerate(picked):
                piece = result[place_in * frame_rows : (place_in + 1) * frame_rows]
                outs = pl.ds(0, STEPS * frame_rows)
                if r - h in seen:
                    acc[r - h, :, outs] = acc[r - h, :, outs] + piece
                else:
                    acc[r - h, :, outs] = piece
                    seen.add(r - h)

    diagonal_seen = set()

    def diagonal(places):
        products(lambda h: stack[REACH + h, REACH], pl.ds(0, width), width, places, diagonal_seen)

    inside = list(range(REACH, REACH + rows))
    outside = [*range(REACH), *range(REACH + rows, rows + 2 * REACH)]
    spread = [halves[n * rows // 4 : (n + 1) * rows // 4] for n in range(4)]
    for quarter in range(3):
        if col_count > 1:
            advance(0, spread[quarter])
        if quarter < 2:
            diagonal(inside[quarter * rows // 2 : (quarter + 1) * rows // 2])

    for way, has_in, place_row in ((0, has_before, 0), (1, has_after, rows + REACH)):

        @pl.when(has_in)
        def _():
            for r in range(REACH):
                halo(way, r).wait_recv()
            shift_rows(place_row, REACH)

        @pl.when(jnp.logical_not(has_in))
        def _():
            for r in range(REACH):
                stack[place_row + r] = jnp.zeros(stack.shape[1:], stack.dtype)

    group = block // col_count
    scale = 1.0 / (frames * rows * ha_count * width)
    lane_block = lax.broadcasted_iota(jnp.int32, (group, channels), 1) // block

    edge_first = (STEPS - REACH) * frame_rows // channels * channels
    edge_pad = (STEPS - REACH) * frame_rows - edge_first
    edge_outs = pl.ds(edge_first, STEPS * frame_rows - edge_first)

    def gather_own_edges():
        if edge_pad:
            edge_own[:edge_pad] = jnp.zeros((edge_pad, channels), edge_own.dtype)
        for step_w in range(STEPS - REACH, STEPS):
            found = gather_edge(lambda r: stack[r, step_w, :, :, edge_tile], rows + 2 * REACH)
            kept = jnp.where(frame_lane % REACH >= 2 * REACH - step_w, found, jnp.zeros_like(found))
            row = edge_pad + (step_w - STEPS + REACH) * frame_rows
            edge_own[row : row + frame_rows] = kept

    def add_edges(owner):
        @pl.when(owner < j)
        def _():
            edge_left[...] = edges[owner].reshape(frame_rows, channels)

        @pl.when(owner > j)
        def _():
            edge_left[...] = -gather_edge(lambda h: others[owner, h, :, :, edge_tile], rows)

        plain = edge_left[...]
        turned_edges = [plain] + [pltpu.roll(plain, REACH * b, axis=1) for b in range(1, STEPS)]
        left = jnp.concatenate(turned_edges, axis=0)
        result = lax.dot_general(
            left, edge_own[...], (((1,), (1,)), ((), ())), preferred_element_type=jnp.float32
        )
        for b in range(STEPS):
            acc[b, :, edge_outs] = acc[b, :, edge_outs] + result[b * frame_rows : (b + 1) * frame_rows]

    def pack(slot):
        def step(step_h, carry):
            moved = {}
            for t in range(frames):
                for g in range(col_count):
                    row = t * block + g * group
                    turn = (g - t) % col_count * block
                    for tile in range(acc.shape[2] // channels):
                        piece = acc[step_h, row : row + group, tile * channels : (tile + 1) * channels]
                        moved[t, g, tile] = pltpu.roll(piece, turn, axis=1) if turn else piece
            for step_w in range(STEPS):
                for step_t in range(STEPS):
                    shift = step_t - REACH
                    base = step_w * frames + shift
                    packed = None
                    for g in range(col_count):
                        total = None
                        for t in range(max(0, -shift), min(frames, frames - shift)):
                            term = moved[t, g, (base + t) // col_count]
                            total = term if total is None else total + term
                        if total is None:
                            total = jnp.zeros((group, channels), jnp.float32)
                        packed = total if packed is None else jnp.where(lane_block == (base + g) % col_count, total, packed)
                    turn = -base % col_count * block
                    packed = pltpu.roll(packed, turn, axis=1) if turn else packed
                    part[slot, step_t * STEPS * STEPS + step_h * STEPS + step_w] = packed
            return carry

        lax.fori_loop(0, STEPS, step, 0, unroll=True)

    def half_slot(owner):
        lanes = pl.ds(pl.multiple_of(jnp.where(owner < j, cut, 0), cut), cut)
        products(lambda h: others[owner, h, :, :, lanes], lanes, cut)
        add_edges(owner)

    turns = [*range(1, half), 0]

    def near_copy(slot, r):
        target = lax.rem(place + r, half)
        return pltpu.make_async_remote_copy(
            src_ref=part.at[slot, pl.ds(first_lag(2 * target + 1 - parity), span)],
            dst_ref=near.at[slot, r],
            send_sem=near_send.at[slot, r],
            recv_sem=near_recv.at[slot, r],
            device_id={"ha": partner},
            device_id_type=MESH,
        )

    def far_copy(slot, r, c):
        target = lax.rem(place + r, half)
        return pltpu.make_async_remote_copy(
            src_ref=mixed.at[slot, r, pieces[c]],
            dst_ref=far.at[slot, r - 1, pieces[c]],
            send_sem=far_send.at[slot, r - 1, c],
            recv_sem=far_recv.at[slot, r - 1, c],
            device_id={"ha": 2 * target + parity},
            device_id_type=MESH,
        )

    def direct_copy(slot, c):
        owner = owner_of(slot)
        return pltpu.make_async_remote_copy(
            src_ref=summed.at[slot, pieces[c]],
            dst_ref=direct.at[j, pieces[c]],
            send_sem=direct_send.at[slot, c],
            recv_sem=direct_recv.at[j, c],
            device_id={"col": owner},
            device_id_type=MESH,
        )

    def direct_arrival(owner, c):
        return pltpu.make_async_remote_copy(
            src_ref=direct.at[owner, pieces[c]],
            dst_ref=direct.at[owner, pieces[c]],
            send_sem=direct_send.at[0, c],
            recv_sem=direct_recv.at[owner, c],
            device_id={"col": owner},
            device_id_type=MESH,
        )

    def turned_copy(slot, c):
        owner = owner_of(slot)
        return pltpu.make_async_remote_copy(
            src_ref=summed.at[slot, pieces[c]],
            dst_ref=turned.at[owner, pieces[c]],
            send_sem=turned_send.at[slot, c],
            recv_sem=turned_recv.at[slot, c],
            device_id={"ha": mirror},
            device_id_type=MESH,
        )

    def pass_near(slot):
        def action():
            for r in turns:
                near_copy(slot, r).start()

        when_active(slot, action)

    def pass_far(slot):
        def action():
            for r in turns:
                target = lax.rem(place + r, half)
                near_copy(slot, r).wait_recv()
                mixed[slot, r] = part[slot, pl.ds(first_lag(2 * target + parity), span)] + near[slot, r]
                if r > 0:
                    far_copy(slot, r, 0).start()
            for c in range(1, len(pieces)):
                for r in range(1, half):
                    far_copy(slot, r, c).start()

        when_active(slot, action)

    def finish(slot):
        def action():
            for c, piece in enumerate(pieces):
                total = mixed[slot, 0, piece]
                for r in range(1, half):
                    far_copy(slot, r, c).wait_recv()
                    total = total + far[slot, r - 1, piece]
                if slot == 0:
                    direct[j, piece] = total
                else:
                    summed[slot, piece] = total
                    direct_copy(slot, c).start()
                    turned_copy(slot, c).start()

        when_active(slot, action)

    if col_count > 1:
        advance(0, spread[3])

    def relay(quarter):
        if col_count > 2:
            advance(1, spread[quarter])

    diagonal(outside)
    pack(0)
    pass_near(0)
    relay(0)
    relay(1)
    gather_own_edges()
    pass_far(0)
    for slot in range(1, col_count):
        owner = owner_of(slot)
        if slot == 1:

            @pl.when(jnp.logical_not(same_side))
            def _():
                half_slot(owner)
                pack(slot)

            pass_near(slot)
            relay(2)
            relay(3)
            pass_far(slot)
            continue
        if slot > 2:

            @pl.when(jnp.logical_not(inner))
            def _():
                pass_far(slot - 1)

            advance(slot - 1, halves)
        if slot == middle + 1:
            for way in range(2):

                @pl.when(receives_rest(way))
                def _():
                    for h in range(rows):
                        arrival(way, rest, h).wait_recv()

        if whole(slot) is None:
            half_slot(owner)
        else:

            @pl.when(whole(slot))
            def _():
                products(lambda h: others[owner, h], pl.ds(0, width), width)

            @pl.when(jnp.logical_not(whole(slot)))
            def _():
                half_slot(owner)

        if slot > 2:

            @pl.when(inner)
            def _():
                pass_far(slot - 1)
                finish(slot - 2)

        pack(slot)
        pass_near(slot)
        if slot > 2:

            @pl.when(jnp.logical_not(inner))
            def _():
                finish(slot - 2)

            if slot == col_count - 1:

                @pl.when(jnp.logical_not(inner))
                def _():
                    finish(slot - 1)

    if col_count > 2:
        pass_far(col_count - 1)

        @pl.when(inner)
        def _():
            finish(col_count - 2)

    elif col_count > 1:
        finish(0)
    else:
        pass_far(0)
    finish(0)
    finish(col_count - 1)

    def assemble(ref, index):
        tiles = [ref[q, index] for q in range(col_count)]
        lines = []
        for g in range(col_count):
            line = None
            for q in range(col_count):
                turn = (q - g) * block % channels
                tile = pltpu.roll(tiles[q], turn, axis=1) if turn else tiles[q]
                line = tile if line is None else jnp.where(lane_block == q, tile, line)
            lines.append(line)
        return lines

    def settle(slot):
        def action():
            for r in turns:
                near_copy(slot, r).wait_send()
                for c in range(len(pieces)):
                    if r > 0:
                        far_copy(slot, r, c).wait_send()

        when_active(slot, action)

    for slot in range(col_count):
        settle(slot)
    for way in range(2):
        for step in range(col_count - 1):

            @pl.when(sends(way, step))
            def _():
                for h in range(rows):
                    hop(way, step, h).wait_send()

        @pl.when(sends_rest(way))
        def _():
            for h in range(rows):
                hop(way, rest, h).wait_send()

    for step in range(col_count - 1):

        @pl.when(sends(0, step))
        def _():
            edge_hop(step).wait_send()

    for way, has in ((0, has_after), (1, has_before)):

        @pl.when(has)
        def _():
            for r in range(REACH):
                halo(way, r).wait_send()

    for slot in range(1, col_count):
        owner = owner_of(slot)
        for c in range(len(pieces)):
            if whole(slot) is None:
                direct_arrival(owner, c).wait_recv()
            else:
                pl.when(jnp.logical_not(whole(slot)))(lambda: direct_arrival(owner, c).wait_recv())
            when_active(slot, lambda: turned_copy(slot, c).wait_recv())

    reach_index = lag_count - 1 - first_lag(i) - first_lag(mirror)
    for base in range(0, span, col_count):
        taken = range(base, min(base + col_count, span))
        lines = []
        for k in taken:
            lines.extend(assemble(turned, jnp.clip(reach_index - k, 0, span - 1)))
        lines.extend([jnp.zeros((group, channels), jnp.float32)] * (channels // group - len(lines)))
        flipped = jnp.concatenate(lines, axis=0).T
        for at, k in enumerate(taken):
            plain = assemble(direct, k)
            for g in range(col_count):
                line = None
                for q in range(col_count):
                    row = q * block + g * group
                    turn = (q - at) * block % channels
                    tile = flipped[row : row + group]
                    tile = pltpu.roll(tile, turn, axis=1) if turn else tile
                    line = tile if line is None else jnp.where(lane_block == q, tile, line)
                out_ref[g * group : (g + 1) * group, k * channels : (k + 1) * channels] = (plain[g] + line) * scale

    def settle_swap(slot):
        def action():
            for c in range(len(pieces)):
                direct_copy(slot, c).wait_send()
                turned_copy(slot, c).wait_send()

        when_active(slot, action)

    for slot in range(1, col_count):
        settle_swap(slot)


def body(ha_count, col_count, features):
    frames, rows, block, width = features.shape
    channels = block * col_count
    lag_count = STEPS**3
    share, span = window_plan(lag_count, channels, ha_count)
    half = ha_count // 2
    group = block // col_count
    dma = pltpu.SemaphoreType.DMA
    lines = max(col_count - 1, 1)
    lanes = -(-STEPS * frames * block // channels) * channels
    tiles = pltpu.VMEM((col_count, span, group, channels), jnp.float32)
    edge_first = (STEPS - REACH) * frames * block // channels * channels
    window = pl.pallas_call(
        functools.partial(kernel, ha_count, col_count),
        out_shape=pltpu.VMEM((block, span * channels), jnp.float32),
        in_specs=[pl.BlockSpec(memory_space=pl.ANY)],
        out_specs=pl.BlockSpec(memory_space=pltpu.VMEM),
        scratch_shapes=[
            pltpu.VMEM((rows + 2 * REACH, STEPS, frames, block, width), features.dtype),
            pltpu.VMEM((col_count, rows, frames, block, width), features.dtype),
            pltpu.VMEM((STEPS, frames * block, lanes), jnp.float32),
            pltpu.VMEM((col_count, lag_count, group, channels), jnp.float32),
            pltpu.VMEM((col_count, half, span, group, channels), jnp.float32),
            pltpu.VMEM((col_count, half, span, group, channels), jnp.float32),
            pltpu.VMEM((col_count, half, span, group, channels), jnp.float32),
            tiles,
            tiles,
            tiles,
            pltpu.VMEM((col_count, frames, block, channels), features.dtype),
            pltpu.VMEM((frames * block, channels), features.dtype),
            pltpu.VMEM((STEPS * frames * block - edge_first, channels), features.dtype),
            dma((rows,)),
            dma((2, REACH)),
            dma((2, REACH)),
            dma((2, lines + 1, rows)),
            dma((2, lines + 1, rows)),
            dma((col_count, half)),
            dma((col_count, half)),
            dma((col_count, half, 2)),
            dma((col_count, half, 2)),
            dma((col_count, 2)),
            dma((col_count, 2)),
            dma((col_count, 2)),
            dma((col_count, 2)),
            dma((lines,)),
            dma((lines,)),
        ],
        compiler_params=pltpu.CompilerParams(collective_id=0, has_side_effects=True),
        name="lag_cov",
    )(features)
    i = lax.axis_index("ha")
    first = jnp.minimum(i * share // channels, lag_count - span)
    return lax.dynamic_slice_in_dim(window, i * share - first * channels, share, 1)


def solution(mesh):
    in_specs = (P(None, "ha", "col", None),)
    out_specs = P("col", "ha")
    counts = (mesh.shape["ha"], mesh.shape["col"])
    return jax.shard_map(
        functools.partial(body, *counts), mesh=mesh, in_specs=in_specs, out_specs=out_specs, check_vma=False
    )
```
